512 devices in a mesh: occ: 16 (over z), vir: 32 (over y, x, core).
Axes of the slice: x: 4, y: 4, z: 16, core: 2. Of those that a mesh axis runs over, the one named last changes fastest.
Arguments:
- amplitudes: bfloat16 [2048, 24576], P('vir', 'occ'), may hold values from -6 to 6
- tiles: bfloat16 [16, 32, 48, 9216], P('occ', 'vir'), may hold values from -0.09375 to 0.09375
- tile_map: int32 [16, 32, 48], P('occ', 'vir'), may hold values from 0 to 128, as said below
Outputs:
- residual: bfloat16 [2048, 24576], P('occ', 'vir')
The draws below stay inside these ranges and needn't reach their ends.
Inputs may be any that keep to these rules, and one draw needn't show every extreme that they name: `tile_map`: in each device's list of 48 slots the live entries name distinct tile pairs and come first; the value 16 * 8 marks an empty slot; some device has all 48 slots live.
All inputs are finite; a program needn't handle non-finite values.
Results may differ from the reference program's by a relative error of at most 0.022.
Values may be sent and summed in bfloat16 or wider, within the bound.
A program may use at most 64 MiB of HBM per device.

```python
import jax
import jax.numpy as jnp
from jax import lax

TILE = 96
CON_TILES = 16
RES_TILES = 8
SLOTS = 48
ROWS = 2048
CD_PAIRS = 24576
AB_PAIRS = 24576
N_OCC = 16
N_VIR = 32


def draw_tile_map(key, part):
    devices = N_OCC * N_VIR
    pairs = CON_TILES * RES_TILES
    keys = jax.random.split(jax.random.fold_in(key, 11), devices)
    orders = jax.vmap(lambda single: jax.random.permutation(single, pairs)[:SLOTS])(keys)
    live = jax.random.randint(jax.random.fold_in(key, 12), (devices,), SLOTS // 5, SLOTS + 1)
    fullest = jax.random.randint(jax.random.fold_in(key, 13), (), 0, devices)
    live = jnp.where(jnp.arange(devices) == fullest, SLOTS, live)
    positions = jnp.arange(SLOTS)
    result = jnp.where(positions[None, :] < live[:, None], orders, pairs)
    return result.reshape(N_OCC, N_VIR, SLOTS).astype(jnp.int32)


def level_of(stream_key, shape, pieces, low, high):
    def one(axis_at, shards_of):
        steps = jax.random.uniform(jax.random.fold_in(jax.random.fold_in(stream_key, 6), axis_at), (shards_of,), jnp.float32, low / len(pieces), high / len(pieces))
        return jnp.repeat(jnp.exp(steps), shape[axis_at] // shards_of).reshape((-1,) + (1,) * (len(shape) - axis_at - 1))

    level = one(*pieces[0])
    for cut in pieces[1:]:
        level = level * one(*cut)
    return level


def noise(stream_key, extent, scale, reach, cuts=(), kind=jnp.bfloat16):
    loudness = level_of(stream_key, extent, cuts, -0.22, 0.18) if cuts else 1.0
    array = jax.random.normal(stream_key, extent, jnp.float32) * scale * loudness
    return jnp.minimum(jnp.maximum(array, -reach), reach).astype(kind)


def setup_inputs(seed: int = 0) -> dict:
    splits = jax.random.split(jax.random.key(seed), 4)
    amplitudes = noise(splits[0], (ROWS, CD_PAIRS), 1.0, 6.0, ((0, 32), (1, 16)))
    tiles = noise(splits[1], (N_OCC, N_VIR, SLOTS, TILE * TILE), (TILE * N_OCC * SLOTS // (2 * RES_TILES)) ** -0.5, 0.09375, ((0, 16), (1, 32)))
    tile_map = draw_tile_map(jax.random.fold_in(splits[3], 71), 0)
    return dict(amplitudes=amplitudes, tiles=tiles, tile_map=tile_map)


def reference(amplitudes, tiles, tile_map):
    pair_ids = jnp.arange(CON_TILES * RES_TILES, dtype=jnp.int32)

    def add_block(running, inputs):
        amp_block, tile_block, map_block = inputs
        onehot = (map_block[:, :, None] == pair_ids[None, None, :]).astype(jnp.float32)
        placed = jnp.einsum("vsp,vsq->vpq", onehot, tile_block.astype(jnp.float32))
        placed = placed.astype(jnp.bfloat16).reshape(N_VIR, CON_TILES, RES_TILES, TILE, TILE)
        placed = placed.transpose(1, 3, 0, 2, 4).reshape(CON_TILES * TILE, N_VIR * RES_TILES * TILE)
        partial_value = jnp.dot(amp_block, placed, preferred_element_type=jnp.float32)
        rounded = lax.optimization_barrier(partial_value.astype(jnp.bfloat16))
        return running + rounded.astype(jnp.float32), None

    amp_blocks = amplitudes.reshape(ROWS, N_OCC, CON_TILES * TILE).transpose(1, 0, 2)
    start_sum = jnp.zeros((ROWS, AB_PAIRS), jnp.float32)
    totals, unused = lax.scan(add_block, start_sum, (amp_blocks, tiles, tile_map))
    return totals.astype(jnp.bfloat16)
```

```python
import jax
import jax.numpy as jnp
from jax import lax
from jax.experimental import pallas as pl
from jax.experimental.pallas import tpu as pltpu
from jax.sharding import PartitionSpec as P

TILE = 96
CON_TILES = 16
RES_TILES = 8
SLOTS = 48
NZ = 16
SIDE = 4
SHARD = 64
DEPTH = CON_TILES * TILE
WIDTH = RES_TILES * TILE
GROUP = 16
HALF = SHARD // 2
COLS = 256
MESH = pl.DeviceIdType.MESH
BF16, F32 = jnp.bfloat16, jnp.float32


def kernel(
    a_hbm, tiles_hbm, map_ref, out_ref,
    a_all, tiles_v, dense, acc, snd, rcv,
    local_sem, line_send, line_recv, plane_send, plane_recv, pair_send, pair_recv, ring_send, ring_recv,
):
    o = lax.axis_index("occ")
    v = lax.axis_index("vir")
    h = lax.rem(v, 2)
    chip = v // 2
    x, y = lax.rem(chip, SIDE), chip // SIDE
    first_x, first_y = 1 - h, h

    def vir_at(dx, dy):
        xx, yy = lax.rem(x + dx + SIDE, SIDE), lax.rem(y + dy + SIDE, SIDE)
        return (yy * SIDE + xx) * 2 + h

    def chip_at(step):
        xx, yy = lax.rem(x + step * first_x, SIDE), lax.rem(y + step * first_y, SIDE)
        return yy * SIDE + xx

    line_up, line_down = vir_at(first_x, first_y), vir_at(-first_x, -first_y)
    plane_up, plane_down = vir_at(first_y, first_x), vir_at(-first_y, -first_x)
    mate = chip * 2 + 1 - h
    ring = (lax.rem(o + 1, NZ), lax.rem(o + NZ - 1, NZ))

    def remote(src, dst, send, recv, device):
        return pltpu.make_async_remote_copy(
            src_ref=src, dst_ref=dst, send_sem=send, recv_sem=recv, device_id=device, device_id_type=MESH
        )

    tiles_copy = pltpu.make_async_copy(tiles_hbm, tiles_v, local_sem.at[0])
    own_copy = pltpu.make_async_copy(a_hbm, a_all.at[chip, h], local_sem.at[1])
    tiles_copy.start()
    own_copy.start()

    barrier = pltpu.get_barrier_semaphore()
    for device in (line_up, line_down, plane_up, plane_down, mate):
        pl.semaphore_signal(barrier, inc=1, device_id={"vir": device}, device_id_type=MESH)
    for device in ring:
        pl.semaphore_signal(barrier, inc=1, device_id={"occ": device}, device_id_type=MESH)
    pl.semaphore_wait(barrier, 7)

    def line_full(k):
        device = line_up if k == 0 else line_down
        return remote(a_hbm, a_all.at[chip, h], line_send.at[k], line_recv.at[k], {"vir": device})

    def line_got(k):
        c = chip_at(3 if k == 0 else 1)
        return c, remote(a_hbm, a_all.at[c, h], line_send.at[k], line_recv.at[k], {"vir": line_up})

    def line_half(k):
        c = chip_at(3 if k == 0 else 1)
        part = a_all.at[c, h, pl.ds(k * HALF, HALF)]
        device = line_up if k == 0 else line_down
        return remote(part, part, line_send.at[2 + k], line_recv.at[2 + k], {"vir": device})

    def line_last(k):
        part = a_all.at[chip_at(2), h, pl.ds(k * HALF, HALF)]
        return remote(part, part, line_send.at[2 + k], line_recv.at[2 + k], {"vir": line_up})

    def where(c):
        xc, yc = lax.rem(c, SIDE), c // SIDE
        mine = y + h * (x - y)
        owner = yc + h * (xc - yc)
        return lax.rem(mine - owner + SIDE, SIDE)

    def plane_full(c, k):
        device = plane_up if k == 0 else plane_down
        part = a_all.at[c, h]
        return remote(part, part, plane_send.at[k, c], plane_recv.at[0, c], {"vir": device})

    def plane_half(c, k):
        device = plane_up if k == 0 else plane_down
        part = a_all.at[c, h, pl.ds(k * HALF, HALF)]
        return remote(part, part, plane_send.at[k, c], plane_recv.at[k, c], {"vir": device})

    def pair(c):
        part = a_all.at[c, h]
        return remote(part, part, pair_send.at[c], pair_recv.at[c], {"vir": mate})

    def pair_got(c):
        part = a_all.at[c, 1 - h]
        return remote(part, part, pair_send.at[c], pair_recv.at[c], {"vir": mate})

    def chunk(r):
        odd = lax.rem(r, 2)
        d = 8 + (1 - 2 * odd) * ((r + 1) // 2)
        return lax.rem(o + d, NZ)

    def plane_out(r):
        c = chunk(r)

        @pl.when(where(c) == 0)
        def _():
            plane_full(c, 0).start()
            plane_full(c, 1).start()
            pair(c).start()

    def plane_in(r):
        c = chunk(r)
        at = where(c)

        @pl.when(at == 1)
        def _():
            plane_full(c, 0).wait_recv()
            plane_half(c, 0).start()
            pair(c).start()

        @pl.when(at == 3)
        def _():
            plane_full(c, 0).wait_recv()
            plane_half(c, 1).start()
            pair(c).start()

        @pl.when(at == 2)
        def _():
            plane_half(c, 0).wait_recv()
            plane_half(c, 1).wait_recv()
            pair(c).start()

    pairs = lax.broadcasted_iota(jnp.int32, (CON_TILES * RES_TILES, SLOTS), 0)
    pairs = (pairs & 15) * RES_TILES + (pairs >> 4)
    select = jnp.where(map_ref[...] == pairs, 1.0, 0.0).astype(BF16)
    row = lax.broadcasted_iota(jnp.int32, (256, 256), 0)
    col = lax.broadcasted_iota(jnp.int32, (256, 256), 1)
    swap = jnp.where(col == (row & 15) * 16 + (row >> 4), 1.0, 0.0).astype(BF16)

    def densify(kb):
        start = pl.multiple_of(kb * GROUP * TILE, GROUP * TILE)
        flat = tiles_v[:, pl.ds(start, GROUP * TILE)]
        placed = jnp.dot(select, flat, preferred_element_type=F32).astype(BF16)
        rows = [
            jnp.concatenate(
                [placed[t * 16:(t + 1) * 16, k * TILE:(k + 1) * TILE] for t in range(RES_TILES)], axis=1
            )
            for k in range(GROUP)
        ]
        mixed = jnp.concatenate(rows, axis=0)
        done = jnp.dot(swap, mixed, preferred_element_type=F32).astype(BF16)
        for c in range(CON_TILES):
            at = pl.multiple_of(c * TILE + kb * GROUP, GROUP)
            dense[pl.ds(at, GROUP), :] = done[c * GROUP:(c + 1) * GROUP, :]

    def densify_range(low, high):
        def body(kb, carry):
            densify(kb)
            return carry

        lax.fori_loop(low, high, body, 0)

    def multiply(c, arm):
        for n in range(0, WIDTH, COLS):
            acc[arm, :, n:n + COLS] = jnp.dot(
                a_all[c].reshape(2 * SHARD, DEPTH), dense[:, n:n + COLS], preferred_element_type=F32
            )

    def hop(arm, s, sub):
        return remote(
            snd.at[arm, s, sub], rcv.at[arm, s, sub], ring_send.at[arm, s, sub], ring_recv.at[arm, s, sub],
            {"occ": ring[arm]},
        )

    def pass_on(arm, s, sub, add):
        value = acc[arm, sub * SHARD:(sub + 1) * SHARD, :]
        if add:
            hop(arm, s - 1, sub).wait_recv()
            value = value + rcv[arm, s - 1, sub].astype(F32)
        snd[arm, s, sub] = value.astype(BF16)
        hop(arm, s, sub).start()

    def ring_step(s, first):
        for arm in (0, 1):
            d = (8 - s) if arm == 0 else (8 + s)
            c = lax.rem(o + d, NZ)
            pair_got(c).wait_recv()
            multiply(c, arm)
        pass_on(0, s, 0, True)
        pass_on(1, s, 1, True)
        pass_on(0, s, 1, not first)
        pass_on(1, s, 0, not first)

    line_full(0).start()
    line_full(1).start()
    tiles_copy.wait()
    densify_range(0, 3)
    for k in (0, 1):
        line_got(k)[1].wait_recv()
        line_half(k).start()
    own_copy.wait()
    densify_range(3, 5)
    for k in (0, 1):
        line_last(k).wait_recv()
    for r in range(4):
        plane_out(r)
    densify_range(5, 6)
    plane_out(4)
    plane_in(0)
    c0 = chunk(0)
    pair_got(c0).wait_recv()
    multiply(c0, 0)
    for arm in (0, 1):
        snd[arm, 0, arm] = acc[0, arm * SHARD:(arm + 1) * SHARD, :].astype(BF16)
        hop(arm, 0, arm).start()

    def plane_body(r, carry):
        @pl.when(r + 4 < NZ)
        def _():
            plane_out(r + 4)

        plane_in(r)
        return carry

    lax.fori_loop(1, 5, plane_body, 0)
    ring_step(1, True)
    lax.fori_loop(5, 7, plane_body, 0)

    def body(s, carry):
        ring_step(s, False)
        lax.fori_loop(jnp.minimum(2 * s + 3, NZ), jnp.minimum(2 * s + 5, NZ), plane_body, 0)
        return carry

    lax.fori_loop(2, 8, body, 0)

    pair_got(o).wait_recv()
    multiply(o, 0)
    for sub in (0, 1):
        hop(0, 7, sub).wait_recv()
        hop(1, 7, sub).wait_recv()
        value = acc[0, sub * SHARD:(sub + 1) * SHARD, :]
        value = value + rcv[0, 7, sub].astype(F32) + rcv[1, 7, sub].astype(F32)
        out_ref[sub * SHARD:(sub + 1) * SHARD, :] = value.astype(BF16)

    for k in (0, 1):
        line_full(k).wait_send()
        line_half(k).wait_send()

    def drain(c, carry):
        at = where(c)
        pair(c).wait_send()

        @pl.when(at == 0)
        def _():
            plane_full(c, 0).wait_send()
            plane_full(c, 1).wait_send()

        @pl.when(at == 1)
        def _():
            plane_half(c, 0).wait_send()

        @pl.when(at == 3)
        def _():
            plane_half(c, 1).wait_send()

        return carry

    lax.fori_loop(0, NZ, drain, 0)
    for arm in (0, 1):
        hop(arm, 0, arm).wait_send()

    def drain_ring(s, carry):
        for arm in (0, 1):
            for sub in (0, 1):
                hop(arm, s, sub).wait_send()
        return carry

    lax.fori_loop(1, 8, drain_ring, 0)


def per_device(amplitudes, tiles, tile_map):
    dma = pltpu.SemaphoreType.DMA
    return pl.pallas_call(
        kernel,
        out_shape=jax.ShapeDtypeStruct((2 * SHARD, WIDTH), BF16),
        in_specs=[
            pl.BlockSpec(memory_space=pl.ANY),
            pl.BlockSpec(memory_space=pl.ANY),
            pl.BlockSpec(memory_space=pltpu.VMEM),
        ],
        out_specs=pl.BlockSpec(memory_space=pltpu.VMEM),
        scratch_shapes=[
            pltpu.VMEM((NZ, 2, SHARD, DEPTH), BF16),
            pltpu.VMEM((SLOTS, TILE * TILE), BF16),
            pltpu.VMEM((DEPTH, WIDTH), BF16),
            pltpu.VMEM((2, 2 * SHARD, WIDTH), F32),
            pltpu.VMEM((2, 8, 2, SHARD, WIDTH), BF16),
            pltpu.VMEM((2, 8, 2, SHARD, WIDTH), BF16),
            dma((2,)),
            dma((4,)),
            dma((4,)),
            dma((2, NZ)),
            dma((2, NZ)),
            dma((NZ,)),
            dma((NZ,)),
            dma((2, 8, 2)),
            dma((2, 8, 2)),
        ],
        compiler_params=pltpu.CompilerParams(
            collective_id=0, has_side_effects=True, vmem_limit_bytes=48 * 1024 * 1024
        ),
    )(amplitudes, tiles.reshape(SLOTS, TILE * TILE), tile_map.reshape(1, SLOTS))


def solution(mesh):
    in_specs = (P("vir", "occ"), P("occ", "vir", None, None), P("occ", "vir", None))
    out_specs = P("occ", "vir")
    return jax.shard_map(
        per_device, mesh=mesh, in_specs=in_specs, out_specs=out_specs, check_vma=False
    )
```

```python
import jax
import jax.numpy as jnp
from jax import lax
from jax.experimental import pallas as pl
from jax.experimental.pallas import tpu as pltpu
from jax.sharding import PartitionSpec as P

TILE = 96
CON_TILES = 16
RES_TILES = 8
SLOTS = 48
NZ = 16
SIDE = 4
SHARD = 64
DEPTH = CON_TILES * TILE
WIDTH = RES_TILES * TILE
GROUP = 16
PIECES = 2
PIECE = SHARD // PIECES
SUBS = 4
SUB = 2 * SHARD // SUBS
AHEAD = 6
EARLY = 3
OTHERS = (1, 3, 2)
COLS = 256
MESH = pl.DeviceIdType.MESH
BF16, F32 = jnp.bfloat16, jnp.float32


def kernel(
    a_hbm, tiles_hbm, map_ref, out_ref,
    a_all, tiles_v, dense, acc, snd, rcv,
    local_sem, line_send, line_recv, plane_send, plane_recv, pair_send, pair_recv, ring_send, ring_recv,
):
    o = lax.axis_index("occ")
    v = lax.axis_index("vir")
    h = lax.rem(v, 2)
    chip = v // 2
    x, y = lax.rem(chip, SIDE), chip // SIDE
    first_x, first_y = 1 - h, h

    def vir_at(dx, dy):
        xx, yy = lax.rem(x + dx, SIDE), lax.rem(y + dy, SIDE)
        return (yy * SIDE + xx) * 2 + h

    def chip_at(step):
        xx, yy = lax.rem(x + step * first_x, SIDE), lax.rem(y + step * first_y, SIDE)
        return yy * SIDE + xx

    def on_line(k):
        return {"vir": vir_at(k * first_x, k * first_y)}

    def on_plane(k):
        return {"vir": vir_at(k * first_y, k * first_x)}

    mate = {"vir": chip * 2 + 1 - h}
    ring = ({"occ": lax.rem(o + 1, NZ)}, {"occ": lax.rem(o + NZ - 1, NZ)})

    def remote(src, dst, send, recv, device):
        return pltpu.make_async_remote_copy(
            src_ref=src, dst_ref=dst, send_sem=send, recv_sem=recv, device_id=device, device_id_type=MESH
        )

    tiles_copy = pltpu.make_async_copy(tiles_hbm, tiles_v, local_sem.at[0])
    own_copy = pltpu.make_async_copy(a_hbm, a_all.at[chip, h], local_sem.at[1])
    tiles_copy.start()
    own_copy.start()

    barrier = pltpu.get_barrier_semaphore()
    for device in [on_line(k) for k in OTHERS] + [on_plane(k) for k in OTHERS] + [mate, *ring]:
        pl.semaphore_signal(barrier, inc=1, device_id=device, device_id_type=MESH)
    pl.semaphore_wait(barrier, 9)

    def rows(p):
        return pl.ds(p * PIECE, PIECE)

    def line(k, p):
        return remote(
            a_hbm.at[rows(p)], a_all.at[chip, h, rows(p)], line_send.at[k, p], line_recv.at[k, p], on_line(k)
        )

    def line_got(c, k, p):
        part = a_all.at[c, h, rows(p)]
        return remote(part, part, line_send.at[k, p], line_recv.at[k, p], on_line(k))

    def plane(c, k, p):
        part = a_all.at[c, h, rows(p)]
        return remote(part, part, plane_send.at[c, k, p], plane_recv.at[c, p], on_plane(k))

    def pair(c):
        part = a_all.at[c, h]
        return remote(part, part, pair_send.at[c], pair_recv.at[c], mate)

    def pair_got(c):
        part = a_all.at[c, 1 - h]
        return remote(part, part, pair_send.at[c], pair_recv.at[c], mate)

    def steps_from(c):
        xc, yc = lax.rem(c, SIDE), c // SIDE
        line_steps = first_x * (x - xc) + first_y * (y - yc)
        plane_steps = first_y * (x - xc) + first_x * (y - yc)
        return lax.rem(line_steps + SIDE, SIDE), lax.rem(plane_steps + SIDE, SIDE)

    def chunk(r):
        odd = lax.rem(r, 2)
        d = 8 + (1 - 2 * odd) * ((r + 1) // 2)
        return lax.rem(o + d, NZ)

    def plane_out(r):
        c = chunk(r)
        near, far = steps_from(c)

        @pl.when(far == 0)
        def _():
            for p in range(PIECES):
                @pl.when(near != 0)
                def _():
                    line_got(c, near, p).wait_recv()

                for k in OTHERS:
                    plane(c, k, p).start()

    def fetch(r):
        c = chunk(r)

        @pl.when(steps_from(c)[1] != 0)
        def _():
            for p in range(PIECES):
                plane(c, 1, p).wait_recv()

        pair(c).start()

    pairs = lax.broadcasted_iota(jnp.int32, (CON_TILES * RES_TILES, SLOTS), 0)
    pairs = (pairs & 15) * RES_TILES + (pairs >> 4)
    select = jnp.where(map_ref[...] == pairs, 1.0, 0.0).astype(BF16)
    row = lax.broadcasted_iota(jnp.int32, (256, 256), 0)
    col = lax.broadcasted_iota(jnp.int32, (256, 256), 1)
    swap = jnp.where(col == (row & 15) * 16 + (row >> 4), 1.0, 0.0).astype(BF16)

    def densify(kb):
        start = pl.multiple_of(kb * GROUP * TILE, GROUP * TILE)
        flat = tiles_v[:, pl.ds(start, GROUP * TILE)]
        placed = jnp.dot(select, flat, preferred_element_type=F32).astype(BF16)
        rows = [
            jnp.concatenate(
                [placed[t * 16:(t + 1) * 16, k * TILE:(k + 1) * TILE] for t in range(RES_TILES)], axis=1
            )
            for k in range(GROUP)
        ]
        mixed = jnp.concatenate(rows, axis=0)
        done = jnp.dot(swap, mixed, preferred_element_type=F32).astype(BF16)
        for c in range(CON_TILES):
            at = pl.multiple_of(c * TILE + kb * GROUP, GROUP)
            dense[pl.ds(at, GROUP), :] = done[c * GROUP:(c + 1) * GROUP, :]

    def densify_range(low, high):
        def body(kb, carry):
            densify(kb)
            return carry

        lax.fori_loop(low, high, body, 0)

    def multiply(c, arm):
        for n in range(0, WIDTH, COLS):
            acc[arm, :, n:n + COLS] = jnp.dot(
                a_all[c].reshape(2 * SHARD, DEPTH), dense[:, n:n + COLS], preferred_element_type=F32
            )

    def hop(arm, s, sub):
        return remote(
            snd.at[arm, s, sub], rcv.at[arm, s, sub], ring_send.at[arm, s, sub], ring_recv.at[arm, s, sub],
            ring[arm],
        )

    def own(arm, sub):
        return acc[arm, sub * SUB:(sub + 1) * SUB, :]

    def pass_on(arm, s, sub, add):
        value = own(arm, sub)
        if add:
            hop(arm, s - 1, sub).wait_recv()
            value = value + rcv[arm, s - 1, sub].astype(F32)
        snd[arm, s, sub] = value.astype(BF16)
        hop(arm, s, sub).start()

    half = SUBS // 2
    long = (tuple(range(half)), tuple(range(half, SUBS)))
    short = (long[1], long[0])

    def ring_step(s, first):
        for arm in (0, 1):
            d = (8 - s) if arm == 0 else (8 + s)
            c = lax.rem(o + d, NZ)
            pair_got(c).wait_recv()
            multiply(c, arm)
        for i in range(half):
            for arm in (0, 1):
                pass_on(arm, s, long[arm][i], True)
        for i in range(half):
            for arm in (0, 1):
                pass_on(arm, s, short[arm][i], not first)

    def each(low, high, f):
        def body(i, carry):
            f(i)
            return carry

        lax.fori_loop(low, high, body, 0)

    def ahead(s):
        each(jnp.minimum(2 * s + AHEAD, NZ), jnp.minimum(2 * s + AHEAD + 2, NZ), plane_out)
        each(2 * s + 1, jnp.minimum(2 * s + 3, NZ), fetch)

    for p in range(PIECES):
        for k in OTHERS:
            line(k, p).start()
    tiles_copy.wait()
    densify_range(0, EARLY)
    own_copy.wait()
    each(0, AHEAD, plane_out)
    densify_range(EARLY, 6)
    fetch(0)
    c0 = chunk(0)
    pair_got(c0).wait_recv()
    multiply(c0, 0)
    for i in range(half):
        for arm in (0, 1):
            sub = long[arm][i]
            snd[arm, 0, sub] = own(0, sub).astype(BF16)
            hop(arm, 0, sub).start()
    ahead(0)
    ring_step(1, True)
    ahead(1)

    def body(s, carry):
        ring_step(s, False)
        ahead(s)
        return carry

    lax.fori_loop(2, 8, body, 0)

    pair_got(o).wait_recv()
    multiply(o, 0)
    for i in range(SUBS):
        sub = (long[0] + long[1])[i]
        hop(0, 7, sub).wait_recv()
        hop(1, 7, sub).wait_recv()
        value = own(0, sub) + rcv[0, 7, sub].astype(F32) + rcv[1, 7, sub].astype(F32)
        out_ref[sub * SUB:(sub + 1) * SUB, :] = value.astype(BF16)

    for p in range(PIECES):
        for k in OTHERS:
            line(k, p).wait_send()

    def drain(c):
        pair(c).wait_send()

        @pl.when(steps_from(c)[1] == 0)
        def _():
            for p in range(PIECES):
                for k in OTHERS:
                    plane(c, k, p).wait_send()

    each(0, NZ, drain)
    for arm in (0, 1):
        for sub in long[arm]:
            hop(arm, 0, sub).wait_send()

    def drain_ring(s):
        for arm in (0, 1):
            for sub in range(SUBS):
                hop(arm, s, sub).wait_send()

    each(1, 8, drain_ring)


def per_device(amplitudes, tiles, tile_map):
    dma = pltpu.SemaphoreType.DMA
    return pl.pallas_call(
        kernel,
        out_shape=jax.ShapeDtypeStruct((2 * SHARD, WIDTH), BF16),
        in_specs=[
            pl.BlockSpec(memory_space=pltpu.HBM),
            pl.BlockSpec(memory_space=pltpu.HBM),
            pl.BlockSpec(memory_space=pltpu.VMEM),
        ],
        out_specs=pl.BlockSpec(memory_space=pltpu.VMEM),
        scratch_shapes=[
            pltpu.VMEM((NZ, 2, SHARD, DEPTH), BF16),
            pltpu.VMEM((SLOTS, TILE * TILE), BF16),
            pltpu.VMEM((DEPTH, WIDTH), BF16),
            pltpu.VMEM((2, 2 * SHARD, WIDTH), F32),
            pltpu.VMEM((2, 8, SUBS, SUB, WIDTH), BF16),
            pltpu.VMEM((2, 8, SUBS, SUB, WIDTH), BF16),
            dma((2,)),
            dma((SIDE, PIECES)),
            dma((SIDE, PIECES)),
            dma((NZ, SIDE, PIECES)),
            dma((NZ, PIECES)),
            dma((NZ,)),
            dma((NZ,)),
            dma((2, 8, SUBS)),
            dma((2, 8, SUBS)),
        ],
        compiler_params=pltpu.CompilerParams(
            collective_id=0, has_side_effects=True, vmem_limit_bytes=61400 * 1024
        ),
    )(amplitudes, tiles.reshape(SLOTS, TILE * TILE), tile_map.reshape(1, SLOTS))


def solution(mesh):
    in_specs = (P("vir", "occ"), P("occ", "vir", None, None), P("occ", "vir", None))
    out_specs = P("occ", "vir")
    return jax.shard_map(
        per_device, mesh=mesh, in_specs=in_specs, out_specs=out_specs, check_vma=False
    )
```

```python
import jax
import jax.numpy as jnp
from jax import lax
from jax.experimental import pallas as pl
from jax.experimental.pallas import tpu as pltpu
from jax.sharding import PartitionSpec as P

TILE = 96
CON_TILES = 16
RES_TILES = 8
SLOTS = 48
NZ = 16
SIDE = 4
SHARD = 64
DEPTH = CON_TILES * TILE
WIDTH = RES_TILES * TILE
GROUP = 16
PIECES = 2
PIECE = SHARD // PIECES
SUBS = 4
SUB = 2 * SHARD // SUBS
OTHERS = (2, 1, 3)
COLS = 256
MESH = pl.DeviceIdType.MESH
BF16, F32 = jnp.bfloat16, jnp.float32


def kernel(
    a_hbm, tiles_hbm, map_hbm, out_hbm,
    a_all, tiles_v, map_ref, result, dense, acc, snd, rcv,
    local_sem, line_send, line_recv, plane_send, plane_recv, pair_send, pair_recv, ring_send, ring_recv,
):
    o = lax.axis_index("occ")
    v = lax.axis_index("vir")
    h = lax.rem(v, 2)
    chip = v // 2
    x, y = lax.rem(chip, SIDE), chip // SIDE
    first_x, first_y = 1 - h, h

    def vir_at(dx, dy):
        xx, yy = lax.rem(x + dx, SIDE), lax.rem(y + dy, SIDE)
        return (yy * SIDE + xx) * 2 + h

    def chip_at(step):
        xx, yy = lax.rem(x + step * first_x, SIDE), lax.rem(y + step * first_y, SIDE)
        return yy * SIDE + xx

    def on_line(k):
        return {"vir": vir_at(k * first_x, k * first_y)}

    def on_plane(k):
        return {"vir": vir_at(k * first_y, k * first_x)}

    mate = {"vir": chip * 2 + 1 - h}
    ring = ({"occ": lax.rem(o + 1, NZ)}, {"occ": lax.rem(o + NZ - 1, NZ)})

    def remote(src, dst, send, recv, device):
        return pltpu.make_async_remote_copy(
            src_ref=src, dst_ref=dst, send_sem=send, recv_sem=recv, device_id=device, device_id_type=MESH
        )

    tiles_copy = pltpu.make_async_copy(tiles_hbm, tiles_v, local_sem.at[0])
    own_copy = pltpu.make_async_copy(a_hbm, a_all.at[chip, h], local_sem.at[1])
    map_copy = pltpu.make_async_copy(map_hbm, map_ref, local_sem.at[2])
    map_copy.start()
    tiles_copy.start()
    own_copy.start()

    barrier = pltpu.get_barrier_semaphore()
    for device in [on_line(k) for k in OTHERS] + [on_plane(k) for k in OTHERS] + [mate, *ring]:
        pl.semaphore_signal(barrier, inc=1, device_id=device, device_id_type=MESH)
    pl.semaphore_wait(barrier, 9)

    def rows(p):
        return pl.ds(p * PIECE, PIECE)

    def line(k, p):
        return remote(
            a_hbm.at[rows(p)], a_all.at[chip, h, rows(p)], line_send.at[k, p], line_recv.at[k, p], on_line(k)
        )

    def line_got(c, k, p):
        part = a_all.at[c, h, rows(p)]
        return remote(part, part, line_send.at[k, p], line_recv.at[k, p], on_line(k))

    def plane(c, k, p):
        part = a_all.at[c, h, rows(p)]
        return remote(part, part, plane_send.at[c, k, p], plane_recv.at[c, p], on_plane(k))

    def pair(c):
        part = a_all.at[c, h]
        return remote(part, part, pair_send.at[c], pair_recv.at[c], mate)

    def pair_got(c):
        part = a_all.at[c, 1 - h]
        return remote(part, part, pair_send.at[c], pair_recv.at[c], mate)

    def steps_from(c):
        xc, yc = lax.rem(c, SIDE), c // SIDE
        line_steps = first_x * (x - xc) + first_y * (y - yc)
        plane_steps = first_y * (x - xc) + first_x * (y - yc)
        return lax.rem(line_steps + SIDE, SIDE), lax.rem(plane_steps + SIDE, SIDE)

    def chunk(r):
        odd = lax.rem(r, 2)
        d = 8 + (1 - 2 * odd) * ((r + 1) // 2)
        return lax.rem(o + d, NZ)

    def fetch(r):
        c = chunk(r)

        @pl.when(steps_from(c)[1] != 0)
        def _():
            for p in range(PIECES):
                plane(c, 1, p).wait_recv()

        pair(c).start()

    def multiply(c, arm):
        for n in range(0, WIDTH, COLS):
            acc[arm, :, n:n + COLS] = jnp.dot(
                a_all[c].reshape(2 * SHARD, DEPTH), dense[:, n:n + COLS], preferred_element_type=F32
            )

    def hop(arm, s, sub):
        return remote(
            snd.at[arm, s, sub], rcv.at[arm, s, sub], ring_send.at[arm, s, sub], ring_recv.at[arm, s, sub],
            ring[arm],
        )

    def own(arm, sub):
        return acc[arm, sub * SUB:(sub + 1) * SUB, :]

    def pass_on(arm, s, sub, add):
        value = own(arm, sub)
        if add:
            hop(arm, s - 1, sub).wait_recv()
            value = value + rcv[arm, s - 1, sub].astype(F32)
        snd[arm, s, sub] = value.astype(BF16)
        hop(arm, s, sub).start()

    half = SUBS // 2
    long = (tuple(range(half)), tuple(range(half, SUBS)))
    short = (long[1], long[0])

    def ring_step(s, first):
        for arm in (0, 1):
            d = (8 - s) if arm == 0 else (8 + s)
            c = lax.rem(o + d, NZ)
            pair_got(c).wait_recv()
            multiply(c, arm)
        for i in range(half):
            for arm in (0, 1):
                pass_on(arm, s, long[arm][i], True)
        for i in range(half):
            for arm in (0, 1):
                pass_on(arm, s, short[arm][i], not first)

    def each(low, high, f):
        def body(i, carry):
            f(i)
            return carry

        lax.fori_loop(low, high, body, 0)

    def rank(c):
        away = lax.rem(c - o + NZ, NZ)
        return jnp.where(away < 8, 15 - 2 * away, 2 * away - 16)

    line_chips = [chip_at(k) for k in range(SIDE)]
    line_ranks = [rank(c) for c in line_chips]
    places = [
        sum((line_ranks[j] < line_ranks[k]).astype(jnp.int32) for j in range(SIDE) if j != k) for k in range(SIDE)
    ]

    def line_out(place):
        @pl.when(places[0] == place)
        def _():
            for p in range(PIECES):
                for k in OTHERS:
                    line(k, p).start()

    def batch_out(place):
        for k in range(SIDE):
            @pl.when(places[k] == place)
            def _():
                for p in range(PIECES):
                    if k != 0:
                        line_got(line_chips[k], SIDE - k, p).wait_recv()
                    for j in OTHERS:
                        plane(line_chips[k], j, p).start()

    def batch_sent(place):
        for k in range(SIDE):
            @pl.when(places[k] == place)
            def _():
                for p in range(PIECES):
                    for j in OTHERS:
                        plane(line_chips[k], j, p).wait_send()

    def next_batch(i):
        batch_sent(i - 1)
        batch_out(i)

    def ahead(s):
        each(2 * s + 1, jnp.minimum(2 * s + 3, NZ), fetch)

    for place in range(SIDE):
        line_out(place)

    pairs = lax.broadcasted_iota(jnp.int32, (CON_TILES * RES_TILES, SLOTS), 0)
    pairs = (pairs & 15) * RES_TILES + (pairs >> 4)
    map_copy.wait()
    select = jnp.where(map_ref[...] == pairs, 1.0, 0.0).astype(BF16)
    row = lax.broadcasted_iota(jnp.int32, (256, 256), 0)
    col = lax.broadcasted_iota(jnp.int32, (256, 256), 1)
    swap = jnp.where(col == (row & 15) * 16 + (row >> 4), 1.0, 0.0).astype(BF16)

    def densify(kb):
        start = pl.multiple_of(kb * GROUP * TILE, GROUP * TILE)
        flat = tiles_v[:, pl.ds(start, GROUP * TILE)]
        placed = jnp.dot(select, flat, preferred_element_type=F32).astype(BF16)
        rows = [
            jnp.concatenate(
                [placed[t * 16:(t + 1) * 16, k * TILE:(k + 1) * TILE] for t in range(RES_TILES)], axis=1
            )
            for k in range(GROUP)
        ]
        mixed = jnp.concatenate(rows, axis=0)
        done = jnp.dot(swap, mixed, preferred_element_type=F32).astype(BF16)
        for c in range(CON_TILES):
            at = pl.multiple_of(c * TILE + kb * GROUP, GROUP)
            dense[pl.ds(at, GROUP), :] = done[c * GROUP:(c + 1) * GROUP, :]

    def densify_range(low, high):
        def body(kb, carry):
            densify(kb)
            return carry

        lax.fori_loop(low, high, body, 0)

    tiles_copy.wait()
    own_copy.wait()
    densify_range(0, 5)
    batch_out(0)
    densify_range(5, 6)
    batch_out(1)
    fetch(0)
    c0 = chunk(0)
    pair_got(c0).wait_recv()
    multiply(c0, 0)
    for i in range(half):
        for arm in (0, 1):
            sub = long[arm][i]
            snd[arm, 0, sub] = own(0, sub).astype(BF16)
            hop(arm, 0, sub).start()
    batch_sent(0)
    batch_out(2)
    ahead(0)
    ring_step(1, True)
    batch_sent(1)
    batch_out(3)
    batch_sent(2)
    ahead(1)

    def body(s, carry):
        ring_step(s, False)
        ahead(s)
        return carry

    lax.fori_loop(2, 8, body, 0)

    pair_got(o).wait_recv()
    multiply(o, 0)
    for p in range(PIECES):
        for k in OTHERS:
            line(k, p).wait_send()

    def drain(c):
        pair(c).wait_send()

    each(0, NZ, drain)
    batch_sent(3)
    for arm in (0, 1):
        for sub in long[arm]:
            hop(arm, 0, sub).wait_send()

    def drain_ring(s):
        for arm in (0, 1):
            for sub in range(SUBS):
                hop(arm, s, sub).wait_send()

    each(1, 7, drain_ring)

    def written(sub):
        part = pl.ds(sub * SUB, SUB)
        return pltpu.make_async_copy(result.at[part], out_hbm.at[part], local_sem.at[3 + sub])

    for i in range(SUBS):
        sub = (long[0] + long[1])[i]
        hop(0, 7, sub).wait_recv()
        hop(1, 7, sub).wait_recv()
        value = own(0, sub) + rcv[0, 7, sub].astype(F32) + rcv[1, 7, sub].astype(F32)
        result[sub * SUB:(sub + 1) * SUB, :] = value.astype(BF16)
        written(sub).start()
    for sub in range(SUBS):
        written(sub).wait()

    each(7, 8, drain_ring)


def per_device(amplitudes, tiles, tile_map):
    dma = pltpu.SemaphoreType.DMA
    return pl.pallas_call(
        kernel,
        out_shape=jax.ShapeDtypeStruct((2 * SHARD, WIDTH), BF16),
        in_specs=[
            pl.BlockSpec(memory_space=pltpu.HBM),
            pl.BlockSpec(memory_space=pltpu.HBM),
            pl.BlockSpec(memory_space=pltpu.HBM),
        ],
        out_specs=pl.BlockSpec(memory_space=pltpu.HBM),
        scratch_shapes=[
            pltpu.VMEM((NZ, 2, SHARD, DEPTH), BF16),
            pltpu.VMEM((SLOTS, TILE * TILE), BF16),
            pltpu.VMEM((1, SLOTS), jnp.int32),
            pltpu.VMEM((2 * SHARD, WIDTH), BF16),
            pltpu.VMEM((DEPTH, WIDTH), BF16),
            pltpu.VMEM((2, 2 * SHARD, WIDTH), F32),
            pltpu.VMEM((2, 8, SUBS, SUB, WIDTH), BF16),
            pltpu.VMEM((2, 8, SUBS, SUB, WIDTH), BF16),
            dma((3 + SUBS,)),
            dma((SIDE, PIECES)),
            dma((SIDE, PIECES)),
            dma((NZ, SIDE, PIECES)),
            dma((NZ, PIECES)),
            dma((NZ,)),
            dma((NZ,)),
            dma((2, 8, SUBS)),
            dma((2, 8, SUBS)),
        ],
        compiler_params=pltpu.CompilerParams(
            collective_id=0, has_side_effects=True, vmem_limit_bytes=61400 * 1024
        ),
    )(amplitudes, tiles.reshape(SLOTS, TILE * TILE), tile_map.reshape(1, SLOTS))


def solution(mesh):
    in_specs = (P("vir", "occ"), P("occ", "vir", None, None), P("occ", "vir", None))
    out_specs = P("occ", "vir")
    return jax.shard_map(
        per_device, mesh=mesh, in_specs=in_specs, out_specs=out_specs, check_vma=False
    )
```

```python
import jax
import jax.numpy as jnp
from jax import lax
from jax.experimental import pallas as pl
from jax.experimental.pallas import tpu as pltpu
from jax.sharding import PartitionSpec as P

TILE = 96
CON_TILES = 16
RES_TILES = 8
SLOTS = 48
NZ = 16
SIDE = 4
SHARD = 64
DEPTH = CON_TILES * TILE
WIDTH = RES_TILES * TILE
GROUP = 16
PIECES = 2
WINDOW = 3
READY = 1
PIECE = SHARD // PIECES
SUBS = 4
SUB = 2 * SHARD // SUBS
OTHERS = (2, 1, 3)
COLS = 256
MESH = pl.DeviceIdType.MESH
BF16, F32 = jnp.bfloat16, jnp.float32


def kernel(
    a_hbm, tiles_hbm, map_hbm, out_hbm,
    a_all, tiles_v, map_ref, result, dense, acc, snd, rcv,
    local_sem, line_send, line_recv, plane_send, plane_recv, pair_send, pair_recv, ring_send, ring_recv,
):
    o = lax.axis_index("occ")
    v = lax.axis_index("vir")
    h = lax.rem(v, 2)
    chip = v // 2
    x, y = lax.rem(chip, SIDE), chip // SIDE
    first_x, first_y = 1 - h, h

    def vir_at(dx, dy):
        xx, yy = lax.rem(x + dx, SIDE), lax.rem(y + dy, SIDE)
        return (yy * SIDE + xx) * 2 + h

    def chip_at(step):
        xx, yy = lax.rem(x + step * first_x, SIDE), lax.rem(y + step * first_y, SIDE)
        return yy * SIDE + xx

    def on_line(k):
        return {"vir": vir_at(k * first_x, k * first_y)}

    def on_plane(k):
        return {"vir": vir_at(k * first_y, k * first_x)}

    mate = {"vir": chip * 2 + 1 - h}
    ring = ({"occ": lax.rem(o + 1, NZ)}, {"occ": lax.rem(o + NZ - 1, NZ)})

    def remote(src, dst, send, recv, device):
        return pltpu.make_async_remote_copy(
            src_ref=src, dst_ref=dst, send_sem=send, recv_sem=recv, device_id=device, device_id_type=MESH
        )

    tiles_copy = pltpu.make_async_copy(tiles_hbm, tiles_v, local_sem.at[0])
    own_copy = pltpu.make_async_copy(a_hbm, a_all.at[chip, h], local_sem.at[1])
    map_copy = pltpu.make_async_copy(map_hbm, map_ref, local_sem.at[2])
    map_copy.start()
    tiles_copy.start()
    own_copy.start()

    barrier = pltpu.get_barrier_semaphore()
    for device in [on_line(k) for k in OTHERS] + [on_plane(k) for k in OTHERS] + [mate, *ring]:
        pl.semaphore_signal(barrier, inc=1, device_id=device, device_id_type=MESH)
    pl.semaphore_wait(barrier, 9)

    def rows(p):
        return pl.ds(p * PIECE, PIECE)

    def line(k, p):
        return remote(
            a_hbm.at[rows(p)], a_all.at[chip, h, rows(p)], line_send.at[k, p], line_recv.at[k, p], on_line(k)
        )

    def line_got(c, k, p):
        part = a_all.at[c, h, rows(p)]
        return remote(part, part, line_send.at[k, p], line_recv.at[k, p], on_line(k))

    def plane(c, k, p):
        part = a_all.at[c, h, rows(p)]
        return remote(part, part, plane_send.at[c, k, p], plane_recv.at[c, p], on_plane(k))

    def pair(c):
        part = a_all.at[c, h]
        return remote(part, part, pair_send.at[c], pair_recv.at[c], mate)

    def pair_got(c):
        part = a_all.at[c, 1 - h]
        return remote(part, part, pair_send.at[c], pair_recv.at[c], mate)

    def steps_from(c):
        xc, yc = lax.rem(c, SIDE), c // SIDE
        line_steps = first_x * (x - xc) + first_y * (y - yc)
        plane_steps = first_y * (x - xc) + first_x * (y - yc)
        return lax.rem(line_steps + SIDE, SIDE), lax.rem(plane_steps + SIDE, SIDE)

    def chunk(r):
        odd = lax.rem(r, 2)
        d = 8 + (1 - 2 * odd) * ((r + 1) // 2)
        return lax.rem(o + d, NZ)

    def fetch(r):
        c = chunk(r)

        @pl.when(steps_from(c)[1] != 0)
        def _():
            for p in range(PIECES):
                plane(c, 1, p).wait_recv()

        pair(c).start()

    def multiply(c, arm):
        for n in range(0, WIDTH, COLS):
            acc[arm, :, n:n + COLS] = jnp.dot(
                a_all[c].reshape(2 * SHARD, DEPTH), dense[:, n:n + COLS], preferred_element_type=F32
            )

    def hop(arm, s, sub):
        return remote(
            snd.at[arm, s, sub], rcv.at[arm, s, sub], ring_send.at[arm, s, sub], ring_recv.at[arm, s, sub],
            ring[arm],
        )

    def own(arm, sub):
        return acc[arm, sub * SUB:(sub + 1) * SUB, :]

    def pass_on(arm, s, sub, add):
        value = own(arm, sub)
        if add:
            hop(arm, s - 1, sub).wait_recv()
            value = value + rcv[arm, s - 1, sub].astype(F32)
        snd[arm, s, sub] = value.astype(BF16)
        hop(arm, s, sub).start()

    half = SUBS // 2
    long = (tuple(range(half)), tuple(range(half, SUBS)))
    short = (long[1], long[0])

    def ring_step(s, first):
        for arm in (0, 1):
            d = (8 - s) if arm == 0 else (8 + s)
            c = lax.rem(o + d, NZ)
            pair_got(c).wait_recv()
            multiply(c, arm)
        for i in range(half):
            for arm in (0, 1):
                pass_on(arm, s, long[arm][i], True)
        for i in range(half):
            for arm in (0, 1):
                pass_on(arm, s, short[arm][i], not first)

    def each(low, high, f):
        def body(i, carry):
            f(i)
            return carry

        lax.fori_loop(low, high, body, 0)

    def rank(c):
        away = lax.rem(c - o + NZ, NZ)
        return jnp.where(away < 8, 15 - 2 * away, 2 * away - 16)

    line_chips = [chip_at(k) for k in range(SIDE)]
    line_ranks = [rank(c) for c in line_chips]
    places = [
        sum((line_ranks[j] < line_ranks[k]).astype(jnp.int32) for j in range(SIDE) if j != k) for k in range(SIDE)
    ]

    def line_out(place):
        @pl.when(places[0] == place)
        def _():
            for p in range(PIECES):
                for k in OTHERS:
                    line(k, p).start()

    def item_out(q):
        place, p = q // PIECES, q % PIECES
        for k in range(SIDE):
            @pl.when(places[k] == place)
            def _():
                if k != 0:
                    line_got(line_chips[k], SIDE - k, p).wait_recv()
                for j in OTHERS:
                    plane(line_chips[k], j, p).start()

    def item_sent(q):
        place, p = q // PIECES, q % PIECES
        for k in range(SIDE):
            @pl.when(places[k] == place)
            def _():
                for j in OTHERS:
                    plane(line_chips[k], j, p).wait_send()

    ITEMS = SIDE * PIECES

    def roll(low, high):
        for q in range(low, high):
            if q < ITEMS:
                item_sent(q)
            if q + WINDOW < ITEMS:
                item_out(q + WINDOW)

    def ahead(s):
        each(2 * s + 1, jnp.minimum(2 * s + 3, NZ), fetch)

    for place in range(SIDE):
        line_out(place)

    pairs = lax.broadcasted_iota(jnp.int32, (CON_TILES * RES_TILES, SLOTS), 0)
    pairs = (pairs & 15) * RES_TILES + (pairs >> 4)
    map_copy.wait()
    select = jnp.where(map_ref[...] == pairs, 1.0, 0.0).astype(BF16)
    row = lax.broadcasted_iota(jnp.int32, (256, 256), 0)
    col = lax.broadcasted_iota(jnp.int32, (256, 256), 1)
    swap = jnp.where(col == (row & 15) * 16 + (row >> 4), 1.0, 0.0).astype(BF16)

    def densify(kb):
        start = pl.multiple_of(kb * GROUP * TILE, GROUP * TILE)
        flat = tiles_v[:, pl.ds(start, GROUP * TILE)]
        placed = jnp.dot(select, flat, preferred_element_type=F32).astype(BF16)
        rows = [
            jnp.concatenate(
                [placed[t * 16:(t + 1) * 16, k * TILE:(k + 1) * TILE] for t in range(RES_TILES)], axis=1
            )
            for k in range(GROUP)
        ]
        mixed = jnp.concatenate(rows, axis=0)
        done = jnp.dot(swap, mixed, preferred_element_type=F32).astype(BF16)
        for c in range(CON_TILES):
            at = pl.multiple_of(c * TILE + kb * GROUP, GROUP)
            dense[pl.ds(at, GROUP), :] = done[c * GROUP:(c + 1) * GROUP, :]

    def densify_range(low, high):
        def body(kb, carry):
            densify(kb)
            return carry

        lax.fori_loop(low, high, body, 0)

    tiles_copy.wait()
    own_copy.wait()
    densify_range(0, 5)
    for q in range(WINDOW):
        item_out(q)
    densify_range(5, 6)
    roll(0, READY)
    fetch(0)
    c0 = chunk(0)
    pair_got(c0).wait_recv()
    multiply(c0, 0)
    for i in range(half):
        for arm in (0, 1):
            sub = long[arm][i]
            snd[arm, 0, sub] = own(0, sub).astype(BF16)
            hop(arm, 0, sub).start()
    roll(READY, READY + PIECES)
    ahead(0)
    ring_step(1, True)
    roll(READY + PIECES, READY + 2 * PIECES)
    ahead(1)

    ring_step(2, False)
    roll(READY + 2 * PIECES, ITEMS)
    ahead(2)

    def body(s, carry):
        ring_step(s, False)
        ahead(s)
        return carry

    lax.fori_loop(3, 8, body, 0)

    pair_got(o).wait_recv()
    multiply(o, 0)
    for p in range(PIECES):
        for k in OTHERS:
            line(k, p).wait_send()

    def drain(c):
        pair(c).wait_send()

    each(0, NZ, drain)
    for arm in (0, 1):
        for sub in long[arm]:
            hop(arm, 0, sub).wait_send()

    def drain_ring(s):
        for arm in (0, 1):
            for sub in range(SUBS):
                hop(arm, s, sub).wait_send()

    each(1, 7, drain_ring)

    def written(sub):
        part = pl.ds(sub * SUB, SUB)
        return pltpu.make_async_copy(result.at[part], out_hbm.at[part], local_sem.at[3 + sub])

    for i in range(SUBS):
        sub = (long[0] + long[1])[i]
        hop(0, 7, sub).wait_recv()
        hop(1, 7, sub).wait_recv()
        value = own(0, sub) + rcv[0, 7, sub].astype(F32) + rcv[1, 7, sub].astype(F32)
        result[sub * SUB:(sub + 1) * SUB, :] = value.astype(BF16)
        written(sub).start()
    for sub in range(SUBS):
        written(sub).wait()

    each(7, 8, drain_ring)


def per_device(amplitudes, tiles, tile_map):
    dma = pltpu.SemaphoreType.DMA
    return pl.pallas_call(
        kernel,
        out_shape=jax.ShapeDtypeStruct((2 * SHARD, WIDTH), BF16),
        in_specs=[
            pl.BlockSpec(memory_space=pltpu.HBM),
            pl.BlockSpec(memory_space=pltpu.HBM),
            pl.BlockSpec(memory_space=pltpu.HBM),
        ],
        out_specs=pl.BlockSpec(memory_space=pltpu.HBM),
        scratch_shapes=[
            pltpu.VMEM((NZ, 2, SHARD, DEPTH), BF16),
            pltpu.VMEM((SLOTS, TILE * TILE), BF16),
            pltpu.VMEM((1, SLOTS), jnp.int32),
            pltpu.VMEM((2 * SHARD, WIDTH), BF16),
            pltpu.VMEM((DEPTH, WIDTH), BF16),
            pltpu.VMEM((2, 2 * SHARD, WIDTH), F32),
            pltpu.VMEM((2, 8, SUBS, SUB, WIDTH), BF16),
            pltpu.VMEM((2, 8, SUBS, SUB, WIDTH), BF16),
            dma((3 + SUBS,)),
            dma((SIDE, PIECES)),
            dma((SIDE, PIECES)),
            dma((NZ, SIDE, PIECES)),
            dma((NZ, PIECES)),
            dma((NZ,)),
            dma((NZ,)),
            dma((2, 8, SUBS)),
            dma((2, 8, SUBS)),
        ],
        compiler_params=pltpu.CompilerParams(
            collective_id=0, has_side_effects=True, vmem_limit_bytes=61400 * 1024
        ),
    )(amplitudes, tiles.reshape(SLOTS, TILE * TILE), tile_map.reshape(1, SLOTS))


def solution(mesh):
    in_specs = (P("vir", "occ"), P("occ", "vir", None, None), P("occ", "vir", None))
    out_specs = P("occ", "vir")
    return jax.shard_map(
        per_device, mesh=mesh, in_specs=in_specs, out_specs=out_specs, check_vma=False
    )
```

```python
import jax
import jax.numpy as jnp
from jax import lax
from jax.experimental import pallas as pl
from jax.experimental.pallas import tpu as pltpu
from jax.sharding import PartitionSpec as P

TILE = 96
CON_TILES = 16
RES_TILES = 8
SLOTS = 48
NZ = 16
SIDE = 4
SHARD = 64
DEPTH = CON_TILES * TILE
WIDTH = RES_TILES * TILE
GROUP = 16
PIECES = 2
WINDOW = 3
READY = 1
PIECE = SHARD // PIECES
SUBS = 4
SUB = 2 * SHARD // SUBS
OTHERS = (2, 1, 3)
COLS = 256
MESH = pl.DeviceIdType.MESH
BF16, F32 = jnp.bfloat16, jnp.float32


def kernel(
    a_hbm, tiles_hbm, map_hbm, out_hbm,
    a_all, tiles_v, map_ref, result, dense, acc, snd, rcv,
    local_sem, line_send, line_recv, plane_send, plane_recv, pair_send, pair_recv, ring_send, ring_recv,
):
    o = lax.axis_index("occ")
    v = lax.axis_index("vir")
    h = lax.rem(v, 2)
    chip = v // 2
    x, y = lax.rem(chip, SIDE), chip // SIDE
    first_x, first_y = 1 - h, h

    def vir_at(dx, dy):
        xx, yy = lax.rem(x + dx, SIDE), lax.rem(y + dy, SIDE)
        return (yy * SIDE + xx) * 2 + h

    def chip_at(step):
        xx, yy = lax.rem(x + step * first_x, SIDE), lax.rem(y + step * first_y, SIDE)
        return yy * SIDE + xx

    def on_line(k):
        return {"vir": vir_at(k * first_x, k * first_y)}

    def on_plane(k):
        return {"vir": vir_at(k * first_y, k * first_x)}

    mate = {"vir": chip * 2 + 1 - h}
    ring = ({"occ": lax.rem(o + 1, NZ)}, {"occ": lax.rem(o + NZ - 1, NZ)})

    def remote(src, dst, send, recv, device):
        return pltpu.make_async_remote_copy(
            src_ref=src, dst_ref=dst, send_sem=send, recv_sem=recv, device_id=device, device_id_type=MESH
        )

    tiles_copy = pltpu.make_async_copy(tiles_hbm, tiles_v, local_sem.at[0])
    own_copy = pltpu.make_async_copy(a_hbm, a_all.at[chip, h], local_sem.at[1])
    map_copy = pltpu.make_async_copy(map_hbm, map_ref, local_sem.at[2])

    barrier = pltpu.get_barrier_semaphore()
    for device in [on_line(k) for k in OTHERS] + [on_plane(k) for k in OTHERS] + [mate, *ring]:
        pl.semaphore_signal(barrier, inc=1, device_id=device, device_id_type=MESH)
    map_copy.start()
    tiles_copy.start()
    own_copy.start()
    pl.semaphore_wait(barrier, 9)

    def rows(p):
        return pl.ds(p * PIECE, PIECE)

    def line(k, p):
        return remote(
            a_hbm.at[rows(p)], a_all.at[chip, h, rows(p)], line_send.at[k, p], line_recv.at[k, p], on_line(k)
        )

    def line_got(c, k, p):
        part = a_all.at[c, h, rows(p)]
        return remote(part, part, line_send.at[k, p], line_recv.at[k, p], on_line(k))

    def plane(c, k, p):
        part = a_all.at[c, h, rows(p)]
        return remote(part, part, plane_send.at[c, k, p], plane_recv.at[c, p], on_plane(k))

    def pair(c):
        part = a_all.at[c, h]
        return remote(part, part, pair_send.at[c], pair_recv.at[c], mate)

    def pair_got(c):
        part = a_all.at[c, 1 - h]
        return remote(part, part, pair_send.at[c], pair_recv.at[c], mate)

    def steps_from(c):
        xc, yc = lax.rem(c, SIDE), c // SIDE
        line_steps = first_x * (x - xc) + first_y * (y - yc)
        plane_steps = first_y * (x - xc) + first_x * (y - yc)
        return lax.rem(line_steps + SIDE, SIDE), lax.rem(plane_steps + SIDE, SIDE)

    def chunk(r):
        odd = lax.rem(r, 2)
        d = 8 + (1 - 2 * odd) * ((r + 1) // 2)
        return lax.rem(o + d, NZ)

    def fetch(r):
        c = chunk(r)

        @pl.when(steps_from(c)[1] != 0)
        def _():
            for p in range(PIECES):
                plane(c, 1, p).wait_recv()

        pair(c).start()

    def multiply(c, arm):
        for n in range(0, WIDTH, COLS):
            acc[arm, :, n:n + COLS] = jnp.dot(
                a_all[c].reshape(2 * SHARD, DEPTH), dense[:, n:n + COLS], preferred_element_type=F32
            )

    def hop(arm, s, sub):
        return remote(
            snd.at[arm, s, sub], rcv.at[arm, s, sub], ring_send.at[arm, s, sub], ring_recv.at[arm, s, sub],
            ring[arm],
        )

    def own(arm, sub):
        return acc[arm, sub * SUB:(sub + 1) * SUB, :]

    def pass_on(arm, s, sub, add):
        value = own(arm, sub)
        if add:
            hop(arm, s - 1, sub).wait_recv()
            value = value + rcv[arm, s - 1, sub].astype(F32)
        snd[arm, s, sub] = value.astype(BF16)
        hop(arm, s, sub).start()

    half = SUBS // 2
    long = (tuple(range(half)), tuple(range(half, SUBS)))
    short = (long[1], long[0])

    def ring_step(s, first):
        for arm in (0, 1):
            d = (8 - s) if arm == 0 else (8 + s)
            c = lax.rem(o + d, NZ)
            pair_got(c).wait_recv()
            multiply(c, arm)
        for i in range(half):
            for arm in (0, 1):
                pass_on(arm, s, long[arm][i], True)
        for i in range(half):
            for arm in (0, 1):
                pass_on(arm, s, short[arm][i], not first)

    def each(low, high, f):
        def body(i, carry):
            f(i)
            return carry

        lax.fori_loop(low, high, body, 0)

    def rank(c):
        away = lax.rem(c - o + NZ, NZ)
        return jnp.where(away < 8, 15 - 2 * away, 2 * away - 16)

    line_chips = [chip_at(k) for k in range(SIDE)]
    line_ranks = [rank(c) for c in line_chips]
    places = [
        sum((line_ranks[j] < line_ranks[k]).astype(jnp.int32) for j in range(SIDE) if j != k) for k in range(SIDE)
    ]

    def line_out(place):
        @pl.when(places[0] == place)
        def _():
            for p in range(PIECES):
                for k in OTHERS:
                    line(k, p).start()

    def item_out(q):
        place, p = q // PIECES, q % PIECES
        for k in range(SIDE):
            @pl.when(places[k] == place)
            def _():
                if k != 0:
                    line_got(line_chips[k], SIDE - k, p).wait_recv()
                for j in OTHERS:
                    plane(line_chips[k], j, p).start()

    def item_sent(q):
        place, p = q // PIECES, q % PIECES
        for k in range(SIDE):
            @pl.when(places[k] == place)
            def _():
                for j in OTHERS:
                    plane(line_chips[k], j, p).wait_send()

    ITEMS = SIDE * PIECES

    def roll(low, high):
        for q in range(low, high):
            if q < ITEMS:
                item_sent(q)
            if q + WINDOW < ITEMS:
                item_out(q + WINDOW)

    def ahead(s):
        each(2 * s + 1, jnp.minimum(2 * s + 3, NZ), fetch)

    for place in range(SIDE):
        line_out(place)

    pairs = lax.broadcasted_iota(jnp.int32, (CON_TILES * RES_TILES, SLOTS), 0)
    pairs = (pairs & 15) * RES_TILES + (pairs >> 4)
    map_copy.wait()
    select = jnp.where(map_ref[...] == pairs, 1.0, 0.0).astype(BF16)
    row = lax.broadcasted_iota(jnp.int32, (256, 256), 0)
    col = lax.broadcasted_iota(jnp.int32, (256, 256), 1)
    swap = jnp.where(col == (row & 15) * 16 + (row >> 4), 1.0, 0.0).astype(BF16)

    def densify(kb):
        start = pl.multiple_of(kb * GROUP * TILE, GROUP * TILE)
        flat = tiles_v[:, pl.ds(start, GROUP * TILE)]
        placed = jnp.dot(select, flat, preferred_element_type=F32).astype(BF16)
        rows = [
            jnp.concatenate(
                [placed[t * 16:(t + 1) * 16, k * TILE:(k + 1) * TILE] for t in range(RES_TILES)], axis=1
            )
            for k in range(GROUP)
        ]
        mixed = jnp.concatenate(rows, axis=0)
        done = jnp.dot(swap, mixed, preferred_element_type=F32).astype(BF16)
        for c in range(CON_TILES):
            at = pl.multiple_of(c * TILE + kb * GROUP, GROUP)
            dense[pl.ds(at, GROUP), :] = done[c * GROUP:(c + 1) * GROUP, :]

    def densify_range(low, high):
        def body(kb, carry):
            densify(kb)
            return carry

        lax.fori_loop(low, high, body, 0)

    tiles_copy.wait()
    own_copy.wait()
    densify_range(0, 5)
    for q in range(WINDOW):
        item_out(q)
    densify_range(5, 6)
    roll(0, READY)
    fetch(0)
    c0 = chunk(0)
    pair_got(c0).wait_recv()
    multiply(c0, 0)
    for i in range(half):
        for arm in (0, 1):
            sub = long[arm][i]
            snd[arm, 0, sub] = own(0, sub).astype(BF16)
            hop(arm, 0, sub).start()
    roll(READY, READY + PIECES)
    ahead(0)
    ring_step(1, True)
    roll(READY + PIECES, READY + 2 * PIECES)
    ahead(1)

    ring_step(2, False)
    roll(READY + 2 * PIECES, ITEMS)
    ahead(2)

    def body(s, carry):
        ring_step(s, False)
        ahead(s)
        return carry

    lax.fori_loop(3, 8, body, 0)

    pair_got(o).wait_recv()
    multiply(o, 0)
    for p in range(PIECES):
        for k in OTHERS:
            line(k, p).wait_send()

    def drain(c):
        pair(c).wait_send()

    each(0, NZ, drain)
    for arm in (0, 1):
        for sub in long[arm]:
            hop(arm, 0, sub).wait_send()

    def drain_ring(s):
        for arm in (0, 1):
            for sub in range(SUBS):
                hop(arm, s, sub).wait_send()

    each(1, 7, drain_ring)

    def written(sub):
        part = pl.ds(sub * SUB, SUB)
        return pltpu.make_async_copy(result.at[part], out_hbm.at[part], local_sem.at[3 + sub])

    for i in range(SUBS):
        sub = (long[0] + long[1])[i]
        hop(0, 7, sub).wait_recv()
        hop(1, 7, sub).wait_recv()
        value = own(0, sub) + rcv[0, 7, sub].astype(F32) + rcv[1, 7, sub].astype(F32)
        result[sub * SUB:(sub + 1) * SUB, :] = value.astype(BF16)
        written(sub).start()
    for sub in range(SUBS):
        written(sub).wait()

    each(7, 8, drain_ring)


def per_device(amplitudes, tiles, tile_map):
    dma = pltpu.SemaphoreType.DMA
    return pl.pallas_call(
        kernel,
        out_shape=jax.ShapeDtypeStruct((2 * SHARD, WIDTH), BF16),
        in_specs=[
            pl.BlockSpec(memory_space=pltpu.HBM),
            pl.BlockSpec(memory_space=pltpu.HBM),
            pl.BlockSpec(memory_space=pltpu.HBM),
        ],
        out_specs=pl.BlockSpec(memory_space=pltpu.HBM),
        scratch_shapes=[
            pltpu.VMEM((NZ, 2, SHARD, DEPTH), BF16),
            pltpu.VMEM((SLOTS, TILE * TILE), BF16),
            pltpu.VMEM((1, SLOTS), jnp.int32),
            pltpu.VMEM((2 * SHARD, WIDTH), BF16),
            pltpu.VMEM((DEPTH, WIDTH), BF16),
            pltpu.VMEM((2, 2 * SHARD, WIDTH), F32),
            pltpu.VMEM((2, 8, SUBS, SUB, WIDTH), BF16),
            pltpu.VMEM((2, 8, SUBS, SUB, WIDTH), BF16),
            dma((3 + SUBS,)),
            dma((SIDE, PIECES)),
            dma((SIDE, PIECES)),
            dma((NZ, SIDE, PIECES)),
            dma((NZ, PIECES)),
            dma((NZ,)),
            dma((NZ,)),
            dma((2, 8, SUBS)),
            dma((2, 8, SUBS)),
        ],
        compiler_params=pltpu.CompilerParams(
            collective_id=0, has_side_effects=True, vmem_limit_bytes=61400 * 1024
        ),
    )(amplitudes, tiles.reshape(SLOTS, TILE * TILE), tile_map.reshape(1, SLOTS))


def solution(mesh):
    in_specs = (P("vir", "occ"), P("occ", "vir", None, None), P("occ", "vir", None))
    out_specs = P("occ", "vir")
    return jax.shard_map(
        per_device, mesh=mesh, in_specs=in_specs, out_specs=out_specs, check_vma=False
    )
```
